32 devices in a mesh: dp: 8 (over y, x, core), tensor: 4 (over z).
Axes of the slice: x: 2, y: 2, z: 4, core: 2. Of those that a mesh axis runs over, the one named last changes fastest.
Arguments:
- inputs: bfloat16 [16384, 768], P('dp'), may hold values from -6 to 6
- w_qkv: bfloat16 [768, 3, 768], P(None, None, 'tensor'), may hold values from -0.3125 to 0.3125
- b_qv: float32 [2, 768], P(None, 'tensor'), may hold values from -3 to 3
- w_out: bfloat16 [768, 768], P('tensor'), may hold values from -1.25 to 1.25
- b_out: float32 [768], replicated, may hold values from -3 to 3
- g_one: float32 [768], replicated, may hold values from 0.5 to 1.5
- s_one: float32 [768], replicated, may hold values from -3 to 3
- w_up: bfloat16 [768, 3072], P(None, 'tensor'), may hold values from -0.21875 to 0.21875
- b_up: float32 [3072], P('tensor'), may hold values from -3 to 3
- w_down: bfloat16 [3072, 768], P('tensor'), may hold values from -0.15625 to 0.15625
- b_down: float32 [768], replicated, may hold values from -3 to 3
- g_two: float32 [768], replicated, may hold values from 0.5 to 1.5
- s_two: float32 [768], replicated, may hold values from -3 to 3
- cotangent: bfloat16 [16384, 768], P('dp'), may hold values from -6 to 6
- pad_mask: int32 [16384], P('dp'), may hold values 0 or 1
- doc_lengths: int32 [32], P('dp'), may hold values from 30 to 512, as said below
Outputs:
- out: bfloat16 [16384, 768], P('dp')
- d_inputs: float32 [16384, 768], P('dp')
- d_w_qkv: float32 [768, 3, 768], P(None, None, 'tensor')
- d_b_qv: float32 [2, 768], P(None, 'tensor')
- d_w_out: float32 [768, 768], P('tensor')
- d_b_out: float32 [768], replicated
- d_g_one: float32 [768], replicated
- d_s_one: float32 [768], replicated
- d_w_up: float32 [768, 3072], P(None, 'tensor')
- d_b_up: float32 [3072], P('tensor')
- d_w_down: float32 [3072, 768], P('tensor')
- d_b_down: float32 [768], replicated
- d_g_two: float32 [768], replicated
- d_s_two: float32 [768], replicated
The draws below stay inside these ranges and needn't reach their ends.
Inputs may be any that keep to these rules, and one draw needn't show every extreme that they name: `doc_lengths`: in every draw one document has 512 true tokens and one has 30. Rows at or beyond a document's count are padding: they are no keys whatever pad_mask says, and their outputs are zero. The first token of a document is always a key.
All inputs are finite; a program needn't handle non-finite values. No bound on the sum of `pad_mask` on one device may be relied on, other than what follows from the above.
Results may differ from the reference program's by a relative error of at most 0.014.
The reference program's roundings to bfloat16 on the way count: a program that leaves them out, or rounds other values in their place, can miss the bound.
Values may be sent and summed in bfloat16 or wider, within the bound.
No kernel may reach another device: no remote copies, remote signals or barrier semaphores. Data moves between devices by JAX's collectives and lax.ppermute only.
A program may use at most 128 MiB of HBM per device.

```python
import jax
import jax.numpy as jnp
from jax import lax

D = 768
HD = 64
HEADS = 12
FF = 3072
L = 512
MIN_LEN = 30
DOCS_DEV = 4
DOCS = 32
TOKENS = 16384
N_DP = 8


def draw_doc_lengths(key, part):
    first, second = jax.random.split(jax.random.fold_in(key, 17))
    counts = jax.random.randint(first, (DOCS,), MIN_LEN, L + 1, dtype=jnp.int32)
    order = jax.random.permutation(second, DOCS)
    counts = counts.at[order[0]].set(L)
    counts = counts.at[order[1]].set(MIN_LEN)
    return counts.astype(jnp.int32)


def set_ends(result, rng, low, high):
    longest = result.shape.index(max(result.shape))
    spots = []
    for shift in (0, 1):
        where = [jax.random.randint(jax.random.fold_in(rng, axis), (), 0, length) for axis, length in enumerate(result.shape)]
        where[longest] = (where[longest] + shift) % result.shape[longest]
        spots.append(tuple(where))
    return result.at[spots[0]].set(low).at[spots[1]].set(high)


def block_scale(own_key, dims, shards, least, top_value):
    level, own = 1.0, jax.random.fold_in(own_key, 6)
    for axis_at, shards_of in shards:
        steps = jnp.exp(jax.random.uniform(jax.random.fold_in(own, axis_at), (shards_of,), jnp.float32, least / len(shards), top_value / len(shards)))
        level = level * jnp.repeat(steps, dims[axis_at] // shards_of).reshape([-1 if axis == axis_at else 1 for axis in range(len(dims))])
    return level


def noise(stream_key, shape, deviation, bound, cuts=(), kind=jnp.bfloat16):
    result = jax.random.normal(stream_key, shape, jnp.float32) * deviation
    if len(cuts) > 0:
        result = block_scale(stream_key, shape, cuts, -0.22, 0.18) * result
    return jnp.clip(result, min=-bound, max=bound).astype(kind)


def setup_inputs(seed: int = 0) -> dict:
    keys = jax.random.split(jax.random.key(seed), 17)
    return {
        "inputs": noise(keys[0], (TOKENS, D), 1.0, 6.0, ((0, 8),)),
        "w_qkv": noise(keys[1], (D, 3, D), (D // 2) ** -0.5, 0.3125, ((2, 4),)),
        "b_qv": noise(keys[2], (2, D), 0.5, 3.0, ((1, 4),), jnp.float32),
        "w_out": noise(keys[3], (D, D), (D // 32) ** -0.5, 1.25, ((0, 4),)),
        "b_out": noise(keys[4], (D,), 0.5, 3.0, (), jnp.float32),
        "g_one": jnp.clip(1.0 + 0.1 * jax.random.normal(keys[5], (D,), jnp.float32), 0.5, 1.5),
        "s_one": noise(keys[6], (D,), 0.5, 3.0, (), jnp.float32),
        "w_up": noise(keys[7], (D, FF), D ** -0.5, 0.21875, ((1, 4),)),
        "b_up": noise(keys[8], (FF,), 0.5, 3.0, ((0, 4),), jnp.float32),
        "w_down": noise(keys[9], (FF, D), (FF // 2) ** -0.5, 0.15625, ((0, 4),)),
        "b_down": noise(keys[10], (D,), 0.5, 3.0, (), jnp.float32),
        "g_two": jnp.clip(1.0 + 0.1 * jax.random.normal(keys[11], (D,), jnp.float32), 0.5, 1.5),
        "s_two": noise(keys[12], (D,), 0.5, 3.0, (), jnp.float32),
        "cotangent": noise(keys[13], (TOKENS, D), 1.0, 6.0, ((0, 8),)),
        "pad_mask": set_ends((jax.random.randint(keys[14], (TOKENS,), 0, 8) < 7).astype(jnp.int32), jax.random.fold_in(keys[14], 1), 0, 1),
        "doc_lengths": draw_doc_lengths(jax.random.fold_in(keys[16], 71), 0),
    }


@jax.custom_vjp
def low(v):
    return lax.optimization_barrier(v.astype(jnp.bfloat16)).astype(jnp.float32)

@jax.custom_vjp
def low_back(v):
    return v

def low_keep(v):
    return (low(v), None)

def low_pass(kept, grad):
    return (grad,)

def back_keep(v):
    return (v, None)

def back_low(kept, grad):
    return (low(grad),)
low.defvjp(low_keep, low_pass)
low_back.defvjp(back_keep, back_low)

def norm_layer(values, gain, shift):
    center = values - lax.optimization_barrier(jnp.mean(values, axis=-1, keepdims=True))
    spread = lax.optimization_barrier(jnp.mean(center * center, axis=-1, keepdims=True))
    return center * lax.rsqrt(spread + 1e-05) * gain + shift

def attend_group(packed):
    queries, key_rows, values, key_valid = packed
    highest = lax.Precision.HIGHEST
    scores = jnp.einsum('gqhe,gkhe->ghqk', queries, key_rows, precision=highest)
    scores = low_back(jnp.where(key_valid[:, None, None, :], scores, -1e+30))
    log_total = jax.nn.logsumexp(scores, axis=-1, keepdims=True)
    weights = low(jnp.exp(scores - log_total))
    return jnp.einsum('ghqk,gkhe->gqhe', weights, values, precision=highest)

def forward(inputs, w_qkv, b_qv, w_out, b_out, g_one, s_one, w_up, b_up, w_down, b_down, g_two, s_two, key_valid, row_weight):
    highest = lax.Precision.HIGHEST
    scale = HD ** (-0.5)
    projected = jnp.einsum('td,dce->tce', inputs, w_qkv, precision=highest)
    queries = low(low_back((projected[:, 0] + b_qv[0]) * scale))
    key_rows = low(low_back(projected[:, 1]))
    values = low(low_back(projected[:, 2] + b_qv[1]))
    shaped = (N_DP, DOCS_DEV, L, HEADS, HD)
    packed = (queries.reshape(shaped), key_rows.reshape(shaped), values.reshape(shaped), key_valid.reshape(N_DP, DOCS_DEV, L))
    context = lax.map(jax.checkpoint(attend_group), packed).reshape(TOKENS, D)
    context = low(low_back(context))
    attn = low_back(jnp.dot(context, w_out, precision=highest))
    h_one = norm_layer(inputs + attn + b_out, g_one, s_one)
    up = low_back(jnp.dot(low(h_one), w_up, precision=highest) + b_up)
    act = low(jax.nn.gelu(up, approximate=False))
    down = low_back(jnp.dot(act, w_down, precision=highest))
    normed = norm_layer(h_one + down + b_down, g_two, s_two)
    return normed * row_weight[:, None]

def reference(inputs, w_qkv, b_qv, w_out, b_out, g_one, s_one, w_up, b_up, w_down, b_down, g_two, s_two, cotangent, pad_mask, doc_lengths):
    position = jnp.arange(L, dtype=jnp.int32)
    inside = position[None, :] < doc_lengths[:, None]
    key_valid = inside & ((pad_mask.reshape(DOCS, L) == 1) | (position[None, :] == 0))
    row_weight = inside.astype(jnp.float32).reshape(TOKENS)
    params = [inputs, w_qkv, b_qv, w_out, b_out, g_one, s_one, w_up, b_up, w_down, b_down, g_two, s_two]
    params = [item.astype(jnp.float32) for item in params]

    def wrapped(*items):
        return forward(*items, key_valid, row_weight)
    normed, pull = jax.vjp(wrapped, *params)
    grads = pull(cotangent.astype(jnp.float32))
    return (normed.astype(jnp.bfloat16), grads[0], grads[1], grads[2], grads[3], grads[4], grads[5], grads[6], grads[7], grads[8], grads[9], grads[10], grads[11], grads[12])
```

```python
import jax
import jax.numpy as jnp
from jax import lax
from jax.sharding import PartitionSpec as P

HD = 64
BF = jnp.bfloat16
F32 = jnp.float32


def norm_layer(values, gain, shift):
    center = values - jnp.mean(values, axis=-1, keepdims=True)
    spread = jnp.mean(center * center, axis=-1, keepdims=True)
    return center * lax.rsqrt(spread + 1e-05) * gain + shift


def gelu_exact(values):
    return jax.nn.gelu(values, approximate=False)


class Links:
    def __init__(self, n_dp, n_t):
        self.n_dp, self.n_t = n_dp, n_t
        self.bits = [1 << b for b in range(n_dp.bit_length() - 1)]
        self.orders = (self.bits[1:], self.bits[:0:-1])

    def swap(self, x, bit):
        return lax.ppermute(x, "dp", [(i, i ^ bit) for i in range(self.n_dp)])

    def shift(self, x, step):
        return lax.ppermute(x, "tensor", [((i + step) % self.n_t, i) for i in range(self.n_t)])

    def spread_plane(self, x):
        half = x.shape[1] // 2
        parts = []
        for order, part in zip(self.orders, (x[:, :half], x[:, half:])):
            slots, held = [0], part[:, None]
            for bit in order:
                held = jnp.concatenate([held, self.swap(held, bit)], axis=1)
                slots = slots + [s | bit for s in slots]
            parts.append(jnp.stack([held[:, slots.index(s)] for s in sorted(slots)], axis=1))
        even = jnp.concatenate(parts, axis=2)
        odd = self.swap(even, 1)
        pieces, _, rows, width = even.shape
        return jnp.stack([even, odd], axis=2).reshape(pieces, self.n_dp, rows, width)

    def sum_plane(self, x):
        pieces, _, rows, width = x.shape
        pairs = x.reshape(pieces, self.n_dp // 2, 2, rows, width)
        held = pairs[:, :, 0] + self.swap(pairs[:, :, 1], 1)
        half = rows // 2
        done = []
        for order, part in zip(self.orders, (held[:, :, :half], held[:, :, half:])):
            slots = list(range(0, self.n_dp, 2))
            for bit in order:
                keep = [s for s in slots if not s & bit]
                kept = jnp.stack([part[:, slots.index(s)] for s in keep], axis=1)
                sent = jnp.stack([part[:, slots.index(s | bit)] for s in keep], axis=1)
                part, slots = kept + self.swap(sent, bit), keep
            done.append(part[:, 0])
        return jnp.concatenate(done, axis=1)

    def gather_weights(self, own):
        others = jnp.stack([self.shift(own[0], k) for k in range(1, self.n_t)])
        return jnp.concatenate([own[None], self.spread_plane(others)], axis=0)

    def sum_grads(self, grads):
        mine = self.sum_plane(grads)
        total = mine[0].astype(F32)
        for k in range(1, self.n_t):
            total = total + self.shift(mine[k], self.n_t - k).astype(F32)
        return self.spread_plane(total.astype(BF)[None])[0]

    def sum_small(self, x):
        for bit in self.bits:
            x = x + self.swap(x, bit)
        bit = 1
        while bit < self.n_t:
            x = x + lax.ppermute(x, "tensor", [(i, i ^ bit) for i in range(self.n_t)])
            bit *= 2
        return x

    def reorder(self, x):
        me = lax.axis_index("dp")
        return jnp.concatenate(
            [lax.dynamic_slice_in_dim(x, me ^ s, 1, axis=0) for s in range(self.n_dp)], axis=0
        )

    def place_docs(self, own):
        me = lax.axis_index("tensor")
        rows = own.shape[0]
        whole = jnp.zeros((self.n_t * rows, own.shape[1]), own.dtype)
        for k in range(self.n_t):
            part = own if k == 0 else self.shift(own, k)
            whole = lax.dynamic_update_slice(whole, part, (((me + k) % self.n_t) * rows, 0))
        return whole


def head_scores(queries, key_rows, key_valid):
    scores = jnp.einsum("nqhe,nkhe->nhqk", queries, key_rows, preferred_element_type=F32)
    return jnp.where(key_valid[:, None, None, :], scores, -1e30)


def per_device(
    n_dp,
    n_t,
    inputs,
    w_qkv,
    b_qv,
    w_out,
    b_out,
    g_one,
    s_one,
    w_up,
    b_up,
    w_down,
    b_down,
    g_two,
    s_two,
    cotangent,
    pad_mask,
    doc_lengths,
):
    links = Links(n_dp, n_t)
    t_index = lax.axis_index("tensor")
    width = inputs.shape[1]
    length = inputs.shape[0] // doc_lengths.shape[0]
    docs = doc_lengths.shape[0] // n_t
    rows = docs * length
    heads = w_qkv.shape[2] // HD
    hidden = w_up.shape[1]
    slot_e = HD // n_dp
    slot_f = hidden // n_dp
    all_heads = heads * n_t
    scale = HD ** (-0.5)

    def own_rows(x):
        return lax.dynamic_slice_in_dim(x, t_index * rows, rows, axis=0)

    x_low = own_rows(inputs)
    d_out = own_rows(cotangent)
    lengths = lax.dynamic_slice_in_dim(doc_lengths, t_index * docs, docs)
    mask = own_rows(pad_mask).reshape(docs, length)
    position = jnp.arange(length, dtype=jnp.int32)
    inside = position[None, :] < lengths[:, None]
    key_valid = inside & ((mask == 1) | (position[None, :] == 0))
    row_weight = inside.astype(F32).reshape(rows, 1)

    w_qkv_t = w_qkv.reshape(width, 3 * heads * HD).T.reshape(3 * heads, n_dp, slot_e, width)
    w_heads = jnp.concatenate([w_qkv_t, w_out.reshape(heads, n_dp, slot_e, width)], axis=0)
    w_heads = w_heads.transpose(1, 0, 2, 3).reshape(n_dp, 4 * heads * slot_e, width)
    own_heads = links.reorder(w_heads)
    own_up = links.reorder(w_up.T.reshape(n_dp, slot_f, width))
    own_down = links.reorder(w_down.reshape(n_dp, slot_f, width))
    biases = jnp.concatenate(
        [
            links.reorder(
                b_qv.reshape(2 * heads, n_dp, slot_e).transpose(1, 0, 2).reshape(n_dp, -1)
            ),
            links.reorder(b_up.reshape(n_dp, slot_f)),
        ],
        axis=1,
    )
    biases = jnp.stack([biases] + [links.shift(biases, k) for k in range(1, n_t)])
    bias_qv = biases[:, :, : 2 * heads * slot_e].reshape(n_t, n_dp, 2, heads, slot_e)
    bias_qv = bias_qv.transpose(2, 0, 3, 1, 4).reshape(2, all_heads * HD)
    bias_up = biases[:, :, 2 * heads * slot_e :].reshape(n_t * hidden)

    all_w = links.gather_weights(own_heads).reshape(n_t, n_dp, 4, heads, slot_e, width)
    all_w = all_w.transpose(2, 0, 3, 1, 4, 5).reshape(4, all_heads * HD, width)
    all_up = links.gather_weights(own_up).reshape(n_t * hidden, width)
    all_down = links.gather_weights(own_down).reshape(n_t * hidden, width)

    def nt(a, b):
        return lax.dot_general(a, b, (((1,), (1,)), ((), ())), preferred_element_type=F32)

    def nn(a, b):
        return lax.dot_general(a, b, (((1,), (0,)), ((), ())), preferred_element_type=F32)

    def tn(a, b):
        return lax.dot_general(a, b, (((0,), (0,)), ((), ())), preferred_element_type=F32)

    shaped = (docs, length, all_heads, HD)
    queries = ((nt(x_low, all_w[0]) + bias_qv[0]) * scale).astype(BF).reshape(shaped)
    key_rows = nt(x_low, all_w[1]).astype(BF).reshape(shaped)
    values = (nt(x_low, all_w[2]) + bias_qv[1]).astype(BF).reshape(shaped)
    scores = head_scores(queries, key_rows, key_valid)
    log_total = jax.nn.logsumexp(scores, axis=-1, keepdims=True)
    prob_low = jnp.exp(scores - log_total).astype(BF)
    context = jnp.einsum("nhqk,nkhe->nqhe", prob_low, values, preferred_element_type=F32)
    context = context.astype(BF).reshape(rows, all_heads * HD)
    z_one = x_low.astype(F32) + nn(context, all_w[3]) + b_out
    h_one, pull_one = jax.vjp(norm_layer, z_one, g_one, s_one)
    h_low = h_one.astype(BF)
    up_value = nt(h_low, all_up) + bias_up
    act, pull_act = jax.vjp(gelu_exact, up_value)
    act_low = act.astype(BF)
    z_two = h_one + nn(act_low, all_down) + b_down
    normed, pull_two = jax.vjp(norm_layer, z_two, g_two, s_two)
    result = links.place_docs((normed * row_weight).astype(BF))

    d_ztwo, d_gtwo, d_stwo = pull_two(d_out.astype(F32) * row_weight)
    d_bdown = jnp.sum(d_ztwo, axis=0)
    dz_two_low = d_ztwo.astype(BF)
    d_wdown = tn(act_low, dz_two_low).astype(BF)
    d_up_low = pull_act(nt(dz_two_low, all_down))[0].astype(BF)
    d_bup = jnp.sum(d_up_low, axis=0, dtype=F32)
    d_wup = tn(d_up_low, h_low).astype(BF)
    ffn_grads = jnp.concatenate(
        [
            d_wup.reshape(n_t, n_dp, slot_f, width),
            d_wdown.reshape(n_t, n_dp, slot_f, width),
        ],
        axis=2,
    )
    ffn_sum = links.reorder(links.sum_grads(ffn_grads))
    d_hone = nn(d_up_low, all_up) + d_ztwo
    d_zone, d_gone, d_sone = pull_one(d_hone)
    d_bout = jnp.sum(d_zone, axis=0)
    dz_one_low = d_zone.astype(BF)
    d_wout = tn(context, dz_one_low).astype(BF)
    d_context = nt(dz_one_low, all_w[3]).astype(BF).reshape(shaped)

    scores = head_scores(*lax.optimization_barrier((queries, key_rows, key_valid)))
    weights = jnp.exp(scores - log_total)
    d_prob = jnp.einsum("nqhe,nkhe->nhqk", d_context, values, preferred_element_type=F32)
    d_values = jnp.einsum(
        "nhqk,nqhe->nkhe", weights.astype(BF), d_context, preferred_element_type=F32
    ).astype(BF)
    inner = jnp.sum(d_prob * weights, axis=-1, keepdims=True)
    d_scores = (weights * (d_prob - inner)).astype(BF)
    d_query = jnp.einsum("nhqk,nkhe->nqhe", d_scores, key_rows, preferred_element_type=F32)
    d_query = d_query.astype(BF) * jnp.asarray(scale, BF)
    d_keys = jnp.einsum("nhqk,nqhe->nkhe", d_scores, queries, preferred_element_type=F32)
    d_keys = d_keys.astype(BF)
    flat = (rows, all_heads * HD)
    stacked = [d_query.reshape(flat), d_keys.reshape(flat), d_values.reshape(flat)]
    d_input = nn(stacked[0], all_w[0]) + nn(stacked[1], all_w[1]) + nn(stacked[2], all_w[2])
    d_inputs = links.place_docs((d_input + d_zone).astype(BF)).astype(F32)
    head_grads = jnp.stack([tn(s, x_low).astype(BF) for s in stacked] + [d_wout])
    head_grads = head_grads.reshape(4, n_t, heads, n_dp, slot_e, width)
    head_grads = head_grads.transpose(1, 3, 0, 2, 4, 5)
    head_grads = head_grads.reshape(n_t, n_dp, 4 * heads * slot_e, width)
    head_sum = links.reorder(links.sum_grads(head_grads))

    d_bqv = jnp.stack(
        [jnp.sum(stacked[0], axis=0, dtype=F32), jnp.sum(stacked[2], axis=0, dtype=F32)]
    )
    d_bqv = d_bqv.reshape(2, n_t, heads, n_dp, slot_e).transpose(1, 3, 0, 2, 4)
    pieces = jnp.concatenate(
        [d_bqv.reshape(n_t, n_dp, -1), d_bup.reshape(n_t, n_dp, slot_f)], axis=2
    )
    pieces = jnp.concatenate(
        [links.reorder(pieces.transpose(1, 0, 2)).transpose(1, 0, 2)] * 2, axis=0
    )
    pieces = lax.dynamic_slice_in_dim(pieces, n_t - t_index, n_t, axis=0)
    common = jnp.stack([d_bout, d_gone, d_sone, d_bdown, d_gtwo, d_stwo])
    small = links.sum_small(jnp.concatenate([common.reshape(-1), pieces.reshape(-1)]))
    common = small[: common.size].reshape(common.shape)
    piece = lax.dynamic_slice_in_dim(
        small[common.size :].reshape(n_t, n_dp, -1), t_index, 1, axis=0
    )[0]
    d_bqv = piece[:, : 2 * heads * slot_e].reshape(n_dp, 2, heads, slot_e)
    d_bqv = d_bqv.transpose(1, 2, 0, 3).reshape(2, heads * HD)
    d_bup = piece[:, 2 * heads * slot_e :].reshape(hidden)

    head_sum = head_sum.reshape(n_dp, 4, heads, slot_e, width).transpose(1, 2, 0, 3, 4)
    head_sum = head_sum.reshape(4, heads * HD, width)
    d_wqkv = head_sum[:3].reshape(3 * heads * HD, width).T.astype(F32)
    return (
        result,
        d_inputs,
        d_wqkv.reshape(width, 3, heads * HD),
        d_bqv,
        head_sum[3].astype(F32),
        common[0],
        common[1],
        common[2],
        ffn_sum[:, :slot_f].reshape(hidden, width).T.astype(F32),
        d_bup,
        ffn_sum[:, slot_f:].reshape(hidden, width).astype(F32),
        common[3],
        common[4],
        common[5],
    )


def solution(mesh):
    n_dp, n_t = mesh.shape["dp"], mesh.shape["tensor"]

    def step(*args):
        return per_device(n_dp, n_t, *args)

    placed = (
        P("dp", None),
        P(None, None, "tensor"),
        P(None, "tensor"),
        P("tensor", None),
        P(),
        P(),
        P(),
        P(None, "tensor"),
        P("tensor"),
        P("tensor", None),
        P(),
        P(),
        P(),
        P("dp", None),
        P("dp"),
        P("dp"),
    )
    return jax.shard_map(
        step,
        mesh=mesh,
        in_specs=placed,
        out_specs=(
            P("dp", None),
            P("dp", None),
            P(None, None, "tensor"),
            P(None, "tensor"),
            P("tensor", None),
            P(),
            P(),
            P(),
            P(None, "tensor"),
            P("tensor"),
            P("tensor", None),
            P(),
            P(),
            P(),
        ),
        check_vma=False,
    )
```
